512 devices in a mesh: cols: 128 (over x, z, core), edge: 4 (over y).
Axes of the slice: x: 4, y: 4, z: 16, core: 2. Of those that a mesh axis runs over, the one named last changes fastest.
Arguments:
- state: float32 [4, 16384, 512], P('edge', 'cols'), may hold values from -6 to 6
- owners: int32 [4, 16384, 1], P('edge', 'cols'), may hold values from 0 to 127; in each aligned block of 128 rows (0 to 127, 128 to 255, ..., all dimensions but the last counted through in order) at most 2 rows name the same one
- orient: int32 [4, 128, 2], P('edge', 'cols'), may hold values from 0 to 1
- crm_state: bfloat16 [4, 128, 58, 16384], P('edge', 'cols'), may hold values from -6 to 6
- active_levels: int32 [4, 128, 256], P('edge', 'cols'), may hold values from 14 to 58
- vertical_map: float32 [58, 64], replicated, may hold values from -0.75 to 0.75
- diffusion: float32 [57], replicated, may hold values from 0.1 to 4
Outputs:
- new_state: float32 [4, 16384, 512], P('edge', 'cols')
- crm_out: bfloat16 [4, 128, 58, 16384], P('edge', 'cols')
The draws below stay inside these ranges and needn't reach their ends.
Inputs may be any that keep to these rules, and one draw needn't show every extreme that they name: `owners`: within the columns of one tile no group is named more than 2 times.
All inputs are finite; a program needn't handle non-finite values.
Results may differ from the reference program's by a relative error of at most 0.001.
Values sent between devices are 32-bit elements; how exact they have to be, the bound alone decides.
A program may use at most 64 MiB of HBM per device.

```python
import math
import jax
import jax.numpy as jnp
import numpy as np
from jax import lax

L = 64
CX = 64
CZ = 58
TW = 8
SUBSTEPS = 2
CPD = 128
EH = 16
FL = 512
CAP = 2
SLOTS = 256
STRIPS = 4
NCOLS = 16384
N_COLS = 128


def set_ends(entries, stream_key, low, high):
    longest = entries.shape.index(max(entries.shape))
    spots = []
    for shift in (0, 1):
        where = [jax.random.randint(jax.random.fold_in(stream_key, axis), (), 0, length) for axis, length in enumerate(entries.shape)]
        where[longest] = (where[longest] + shift) % entries.shape[longest]
        spots.append(tuple(where))
    return entries.at[spots[0]].set(low).at[spots[1]].set(high)


def level_of(key, shape, split, least, largest):
    gain, own = 1.0, jax.random.fold_in(key, 6)
    for dim, parts in split:
        draws = jnp.exp(jax.random.uniform(jax.random.fold_in(own, dim), (parts,), jnp.float32, least / len(split), largest / len(split)))
        gain = gain * jnp.repeat(draws, shape[dim] // parts).reshape([-1 if axis == dim else 1 for axis in range(len(shape))])
    return gain


def routed_block(own_key, own, number, rows, number_of, top, reach, lean):
    order = jax.random.permutation(own_key, number_of)
    crowded, usual = load_shares(number_of, rows * top, reach, lean, True), load_shares(number_of, rows * top, reach, lean, False)
    places = jnp.arange(number_of)

    def named(sizes, offset_by):
        used = int((sizes > 0).sum())
        fixed = max(1, used // 4)
        moved = fixed + (places - fixed + offset_by * (used - fixed)) % max(1, number_of - fixed)
        return jnp.zeros((number_of,), jnp.int32).at[order[jnp.where(places < fixed, places, moved)]].set(jnp.asarray(sizes, jnp.int32))

    sizes = jnp.where(number % 4 == 0, named(crowded, number // 4), named(usual, number - number // 4 - 1))
    mixed = jax.random.permutation(jax.random.fold_in(own, 3), number_of)
    source_of, taker = mixed[0:number_of // 2 * 2:2], mixed[1:number_of // 2 * 2:2]
    margin = jnp.minimum(sizes[source_of] - 1, reach - sizes[taker]) // 2
    margin = jnp.where((source_of == order[0]) | (taker == order[0]) | (sizes[taker] == 0), 0, jnp.maximum(margin, 0))
    moved = jax.random.randint(jax.random.fold_in(own, 4), (number_of // 2,), 0, 1 << 20) % (margin + 1)
    sizes = sizes.at[source_of].add(-moved).at[taker].add(moved)
    labels = jnp.searchsorted(jnp.cumsum(sizes), jnp.arange(rows * top), side="right").astype(jnp.int32)
    listing = labels.reshape(top, rows).T
    listing = listing[jax.random.permutation(jax.random.fold_in(own, 1), rows)]
    offset_by = jax.random.randint(jax.random.fold_in(own, 2), (rows, 1), 0, top)
    return jnp.take_along_axis(listing, (jnp.arange(top)[None, :] + offset_by) % top, axis=1)


def load_shares(count, total, limit, slope, full):
    portions = [(1 << 20) // math.isqrt(standing ** slope) + 1 for standing in range(1, count + 1)]
    largest = limit if full else min(limit, max(-(-total // count), total * portions[0] // sum(portions)))
    least = 1 if total - largest >= count - 1 else 0
    given, spare = [largest] + [least] * (count - 1), total - largest - least * (count - 1)
    while spare > 0:
        movable = [i for i in range(1, count) if given[i] < largest] or [i for i in range(1, count) if given[i] < limit]
        pool, remaining = sum([portions[i] for i in movable]), spare
        for i in movable:
            addition = min(limit - given[i], max(1, remaining * portions[i] // pool), spare)
            given[i] = given[i] + addition
            spare = spare - addition
    return np.array(given)


def normal_values(key, dims, width, reach, pieces=(), kind=jnp.bfloat16):
    array = jax.random.normal(key, dims, jnp.float32) * width
    if len(pieces) > 0:
        array = level_of(key, dims, pieces, -0.22, 0.18) * array
    return jnp.clip(array, min=-reach, max=reach).astype(kind)


def setup_inputs(seed: int = 0) -> dict:
    key_of = jax.random.split(jax.random.key(seed), 8)
    state = normal_values(key_of[0], (STRIPS, NCOLS, FL), 1.0, 6.0, ((0, 4), (1, 128)), jnp.float32)
    owners_keys = jax.random.split(jax.random.fold_in(key_of[1], 1), STRIPS * NCOLS // CPD)
    owners_turns = jax.random.permutation(jax.random.fold_in(key_of[1], 3), STRIPS * NCOLS // CPD)
    owners = jax.vmap(lambda own, number: routed_block(jax.random.fold_in(key_of[1], 2), own, number, CPD, N_COLS, 1, CAP, 2))(owners_keys, owners_turns).reshape((STRIPS, NCOLS, 1))
    orient = set_ends(jax.random.randint(key_of[2], (STRIPS, N_COLS, 2), 0, 2), jax.random.fold_in(key_of[2], 1), 0, 1).astype(jnp.int32)
    crm_state = normal_values(key_of[3], (STRIPS, N_COLS, CZ, CX * SLOTS), 1.0, 6.0, ((0, 4), (1, 128)))
    active_levels = set_ends(jax.random.randint(key_of[4], (STRIPS, N_COLS, SLOTS), CZ // 4, CZ + 1), jax.random.fold_in(key_of[4], 1), CZ // 4, CZ).astype(jnp.int32)
    vertical_map = normal_values(key_of[5], (CZ, L), L ** -0.5, 0.75, (), jnp.float32)
    diffusion = jnp.clip(jnp.exp(jax.random.uniform(key_of[6], (CZ - 1,), jnp.float32, math.log(0.1), math.log(4.0))), 0.1, 4.0)
    return dict(state=state, owners=owners, orient=orient, crm_state=crm_state, active_levels=active_levels, vertical_map=vertical_map, diffusion=diffusion)


kappa_edge = 0.25
max_courant = 0.9
relax_rate = 0.5


def factorize(lower, diagonal, upper):
    depth = diagonal.shape[0]
    prev_c = jnp.zeros(diagonal.shape[1:], jnp.float32)
    factors = []
    denoms = []
    for level in range(depth):
        denom = diagonal[level] + lower[level] * prev_c
        prev_c = -upper[level] / denom
        factors.append(prev_c)
        denoms.append(denom)
    return factors, denoms


def tridiag(lower, factors, denoms, values):
    depth = values.shape[0]
    prev_d = jnp.zeros(values.shape[1:], jnp.float32)
    offsets = []
    for level in range(depth):
        prev_d = (values[level] + lower[level][None, :] * prev_d) / denoms[level][None, :]
        offsets.append(prev_d)
    after = jnp.zeros(values.shape[1:], jnp.float32)
    solved = [None] * depth
    for level in range(depth - 1, -1, -1):
        after = offsets[level] - factors[level][None, :] * after
        solved[level] = after
    return jnp.stack(solved, axis=0)


def physics(columns, crm_slab, active_count, vertical_map, diffusion):
    slots = columns.shape[0]
    temper = columns[:, 0:L]
    moisture = columns[:, L:2 * L]
    forcing = jnp.einsum("zl,sl->zs", vertical_map, temper, precision=lax.Precision.HIGHEST, preferred_element_type=jnp.float32)
    courant = max_courant * jax.nn.sigmoid(jnp.einsum("zl,sl->zs", vertical_map, moisture, precision=lax.Precision.HIGHEST, preferred_element_type=jnp.float32))
    field = crm_slab.reshape(CZ, CX, slots).astype(jnp.float32)
    mean_before = jnp.mean(field, axis=1)
    spread_before = jnp.mean(field * field, axis=1) - mean_before * mean_before
    field = field + relax_rate * (forcing - mean_before)[:, None, :]
    heights = jnp.arange(CZ - 1, dtype=jnp.int32)
    coupled = (heights[:, None] + 1 < active_count[None, :]).astype(jnp.float32)
    interfaces = diffusion[:, None] * coupled
    zero_row = jnp.zeros((1, slots), jnp.float32)
    lower = jnp.concatenate([zero_row, interfaces], axis=0)
    upper = jnp.concatenate([interfaces, zero_row], axis=0)
    diagonal = 1.0 + lower + upper
    factors, denoms = factorize(lower, diagonal, upper)
    for substep in range(SUBSTEPS):
        field = field - courant[:, None, :] * (field - jnp.roll(field, 1, axis=1))
        field = tridiag(lower, factors, denoms, field)
    mean_after = jnp.mean(field, axis=1)
    spread_after = jnp.mean(field * field, axis=1) - mean_after * mean_after
    tend_mean = jnp.einsum("zs,zl->sl", mean_after - mean_before, vertical_map, precision=lax.Precision.HIGHEST, preferred_element_type=jnp.float32)
    tend_spread = jnp.einsum("zs,zl->sl", spread_after - spread_before, vertical_map, precision=lax.Precision.HIGHEST, preferred_element_type=jnp.float32)
    tend = jnp.concatenate([tend_mean, tend_spread], axis=1)
    return tend, field.reshape(CZ, CX * slots).astype(jnp.bfloat16)


def fill_slots(index, rows):
    return jnp.zeros((N_COLS * SLOTS, 2 * L), jnp.float32).at[index].set(rows)


def pick_rows(table, index):
    return table[index]


def reference(state, owners, orient, crm_state, active_levels, vertical_map, diffusion):
    tiles = state.reshape(STRIPS, N_COLS, EH, TW, FL)
    upper_row = tiles[:, :, EH - 1]
    lower_row = tiles[:, :, 0]
    ghost_low = jnp.roll(upper_row, 1, axis=0)
    ghost_high = jnp.roll(lower_row, -1, axis=0)
    flip_low = (orient[:, :, 0] == 1)[:, :, None, None]
    flip_high = (orient[:, :, 1] == 1)[:, :, None, None]
    ghost_low = jnp.where(flip_low, ghost_low[:, :, ::-1], ghost_low)
    ghost_high = jnp.where(flip_high, ghost_high[:, :, ::-1], ghost_high)
    padded = jnp.concatenate([ghost_low[:, :, None], tiles, ghost_high[:, :, None]], axis=2)
    moved = tiles + kappa_edge * ((padded[:, :, 2:] + padded[:, :, :-2]) - 2.0 * tiles)
    moved = moved.reshape(STRIPS, N_COLS, CPD, FL)
    group_of = owners.reshape(STRIPS, N_COLS, CPD)
    same = group_of[..., :, None] == group_of[..., None, :]
    order = jnp.arange(CPD, dtype=jnp.int32)
    earlier = order[None, :] < order[:, None]
    ranking = jnp.sum((same & earlier).astype(jnp.int32), axis=-1).astype(jnp.int32)
    source = jnp.arange(N_COLS, dtype=jnp.int32)[None, :, None]
    flat_index = (group_of * SLOTS + source * CAP + ranking).astype(jnp.int32)
    used = moved[..., 0:2 * L]
    buffers = jax.vmap(fill_slots)(flat_index.reshape(STRIPS, N_COLS * CPD), used.reshape(STRIPS, N_COLS * CPD, 2 * L))

    def run(items):
        columns, slab, counts = items
        return physics(columns, slab, counts, vertical_map, diffusion)

    tends, crm_new = lax.map(run, (buffers.reshape(STRIPS * N_COLS, SLOTS, 2 * L), crm_state.reshape(STRIPS * N_COLS, CZ, CX * SLOTS), active_levels.reshape(STRIPS * N_COLS, SLOTS)))
    picked = jax.vmap(pick_rows)(tends.reshape(STRIPS, N_COLS * SLOTS, 2 * L), flat_index.reshape(STRIPS, N_COLS * CPD))
    moved = moved.reshape(STRIPS, N_COLS * CPD, FL)
    new_state = jnp.concatenate([moved[..., 0:2 * L] + picked, moved[..., 2 * L:]], axis=2)
    return new_state, crm_new.reshape(STRIPS, N_COLS, CZ, CX * SLOTS)
```

```python
import functools

import jax
import jax.numpy as jnp
from jax import lax
from jax.experimental import pallas as pl
from jax.experimental.pallas import tpu as pltpu
from jax.sharding import PartitionSpec as P

MESH = pl.DeviceIdType.MESH

L = 64
CX = 64
CZ = 58
TW = 8
CPD = 128
FL = 512
SLOTS = 256
HALF = 128
N = 128
NX, NZ, NC, NE = 4, 16, 2, 4
ZROWS = 64
HROWS = ZROWS * CX

kappa_edge = 0.25
max_courant = 0.9
relax_rate = 0.5

HIGHEST = lax.Precision.HIGHEST


def index_of(x, z, core):
    return (x * NZ + z) * NC + core


def around(value, count):
    return lax.rem(value + count, count)


def split(values):
    high = values.astype(jnp.bfloat16)
    low = (values - high.astype(jnp.float32)).astype(jnp.bfloat16)
    return jnp.concatenate([high, low], axis=1)


def kernel(
    state_hbm, owners_hbm, orient_hbm, crm_hbm, active_hbm, vmap_hbm, diff_hbm,
    new_hbm, out_hbm,
    tile, ghosts, owner, active, vmap, orient, diff, crm, field,
    rl, cl, el, ru, cu, eu, a1, b1, d1, a2, b2, mean, spread, part, partsq,
    weights, delta, moved, send, recv, reply, ret,
    ready, load_sem, crm_sem, halo_send, halo_recv, fwd_send, fwd_recv, rep_send, rep_recv, store_sem, crm_out_sem,
):
    me = lax.axis_index("cols")
    strip = lax.axis_index("edge")
    x = me // (NZ * NC)
    z = lax.rem(me // NC, NZ)
    core = lax.rem(me, NC)
    above = around(strip + 1, NE)
    below = around(strip - 1, NE)

    barrier = pltpu.get_barrier_semaphore()

    def greet(column, row):
        pl.semaphore_signal(barrier, inc=1, device_id=(column, row), device_id_type=MESH)

    def greet_ring(i, carry):
        greet(index_of(x, around(z + i, NZ), core), strip)
        return carry

    def plane_peer(i):
        i = i + core + NC * x
        return index_of(lax.rem(i // NC, NX), z, lax.rem(i, NC))

    def greet_plane(i, carry):
        greet(plane_peer(i), strip)
        return carry

    lax.fori_loop(1, NZ, greet_ring, 0)
    lax.fori_loop(1, NX * NC, greet_plane, 0)
    greet(me, above)
    greet(me, below)

    loads = [
        pltpu.make_async_copy(state_hbm.at[0], tile.at[pl.ds(TW, CPD)], load_sem.at[0]),
        pltpu.make_async_copy(owners_hbm, owner, load_sem.at[1]),
        pltpu.make_async_copy(active_hbm, active, load_sem.at[2]),
        pltpu.make_async_copy(vmap_hbm, vmap, load_sem.at[3]),
        pltpu.make_async_copy(orient_hbm, orient, load_sem.at[4]),
        pltpu.make_async_copy(diff_hbm, diff, load_sem.at[5]),
    ]
    for load in loads:
        load.start()
    pieces = 4
    width = CX * SLOTS // pieces
    crm_loads = [
        pltpu.make_async_copy(
            crm_hbm.at[0, 0, :, pl.ds(i * width, width)], crm.at[:, pl.ds(i * width, width)], crm_sem.at[i]
        )
        for i in range(pieces)
    ]
    for load in crm_loads:
        load.start()
    for load in loads:
        load.wait()

    count = active[...]

    def put(ref, level, values):
        for half in range(2):
            ref[pl.ds(half * ZROWS + level, 1), :] = values[:, half * HALF : (half + 1) * HALF]

    def factor(i, carry):
        lower_e, upper_e, k_before, k_after = carry
        level = i
        k_here = jnp.where(level + 1 < count, diff[0, jnp.minimum(level, CZ - 2)], 0.0)
        k_here = jnp.where(level < CZ - 1, k_here, 0.0)
        inv = 1.0 / (1.0 + k_before + k_here - k_before * lower_e)
        lower_e = k_here * inv
        put(rl, level, inv)
        put(cl, level, k_before * inv)
        put(el, level, lower_e)
        top = CZ - 1 - i
        k_under = jnp.where(top < count, diff[0, jnp.maximum(top - 1, 0)], 0.0)
        k_under = jnp.where(top > 0, k_under, 0.0)
        inv_u = 1.0 / (1.0 + k_after + k_under - k_after * upper_e)
        upper_e = k_under * inv_u
        put(ru, top, inv_u)
        put(cu, top, k_after * inv_u)
        put(eu, top, upper_e)
        return lower_e, upper_e, k_here, k_under

    zero_row = jnp.zeros((1, SLOTS), jnp.float32)
    lax.fori_loop(0, CZ, factor, (zero_row, zero_row, zero_row, zero_row))

    weights[...] = jnp.zeros((CPD, CPD), jnp.float32)
    weights[0:CZ, 0:L] = vmap[...]
    weights[L : L + CZ, L : 2 * L] = vmap[...]
    delta[...] = jnp.zeros((CPD, SLOTS), jnp.float32)

    sums = tuple(jnp.zeros((CZ, HALF), jnp.float32) for _ in range(4))

    def relayout(column, carry):
        carry = list(carry)
        spot = lax.rem(column, 8) * 8 + column // 8
        for half in range(2):
            start = pl.multiple_of(column * SLOTS + half * HALF, HALF)
            values = crm[:, pl.ds(start, HALF)].astype(jnp.float32)
            carry[half] = carry[half] + values
            carry[2 + half] = carry[2 + half] + values * values
            for block in range(ZROWS // 8):
                rows = min(8, CZ - 8 * block)
                field[pl.ds(half * HROWS + block * 8 * CX + spot, rows, stride=CX), :] = values[8 * block : 8 * block + rows]
        return tuple(carry)

    for i in range(pieces):
        crm_loads[i].wait()
        sums = lax.fori_loop(i * CX // pieces, (i + 1) * CX // pieces, relayout, sums)
    for half in range(2):
        levels = slice(half * ZROWS, half * ZROWS + CZ)
        average = sums[half] * (1.0 / CX)
        mean[levels, :] = average
        spread[levels, :] = sums[2 + half] * (1.0 / CX) - average * average

    group = owner[...]
    line = lax.broadcasted_iota(jnp.int32, (CPD, CPD), 0)
    along = lax.broadcasted_iota(jnp.int32, (CPD, CPD), 1)
    named = jnp.where(line == group, 1.0, 0.0)
    earlier = jnp.where(line < along, 1.0, 0.0)
    before = jnp.dot(named.astype(jnp.bfloat16), earlier.astype(jnp.bfloat16), preferred_element_type=jnp.float32)
    rank = jnp.sum(named * before, axis=0, keepdims=True)
    slot = group * 2 + rank.astype(jnp.int32)
    picks = jnp.where(lax.broadcasted_iota(jnp.int32, (SLOTS, CPD), 0) == slot, 1.0, 0.0).astype(jnp.bfloat16)

    pl.semaphore_wait(barrier, NZ - 1 + NX * NC - 1 + 2)

    def announce(i, carry):
        pl.semaphore_signal(ready, inc=1, device_id=(plane_peer(i), strip), device_id_type=MESH)
        return carry

    upward = pltpu.make_async_remote_copy(
        state_hbm.at[0, pl.ds(CPD - TW, TW)], ghosts.at[0], halo_send.at[0], halo_recv.at[0],
        device_id=(me, above), device_id_type=MESH,
    )
    downward = pltpu.make_async_remote_copy(
        state_hbm.at[0, pl.ds(0, TW)], ghosts.at[1], halo_send.at[1], halo_recv.at[1],
        device_id=(me, below), device_id_type=MESH,
    )
    upward.start()
    downward.start()
    lax.fori_loop(1, NX * NC, announce, 0)
    upward.wait()
    downward.wait()
    for side in range(2):
        flip = orient[0, side] == 1
        for w in range(TW):
            row = side * (TW + CPD) + w
            tile[row : row + 1, :] = jnp.where(flip, ghosts[side, TW - 1 - w : TW - w, :], ghosts[side, w : w + 1, :])

    def step(lanes):
        here = tile[TW : TW + CPD, lanes]
        return here + kappa_edge * ((tile[2 * TW : 2 * TW + CPD, lanes] + tile[0:CPD, lanes]) - 2.0 * here)

    used = step(slice(0, 2 * L))
    moved[:, 0 : 2 * L] = used
    both = jnp.dot(picks, split(used), preferred_element_type=jnp.float32)
    send[...] = (both[:, 0 : 2 * L] + both[:, 2 * L :]).reshape(N, 2, 2 * L)
    pl.semaphore_wait(ready, NX * NC - 1)

    def far(i):
        return (1 - 2 * lax.rem(i, 2)) * ((i + 1) // 2)

    def forward(i, carry):
        ring, plane = i // (NX * NC), lax.rem(i, NX * NC)
        peer = index_of(
            around(x + NX // 2 + far(plane // NC), NX),
            around(z + NZ // 2 + far(ring), NZ),
            lax.rem(core + 1 - lax.rem(plane, NC), NC),
        )
        pltpu.make_async_remote_copy(
            send.at[peer], recv.at[me], fwd_send, fwd_recv.at[x // 2], device_id=(peer, strip), device_id_type=MESH
        ).start()
        return carry

    lax.fori_loop(0, N - 1, forward, 0)
    pltpu.make_async_copy(send.at[me], recv.at[me], fwd_recv.at[x // 2]).start()

    moved[:, 2 * L :] = step(slice(2 * L, FL))
    rest = pltpu.make_async_copy(moved.at[:, pl.ds(2 * L, FL - 2 * L)], new_hbm.at[0, :, pl.ds(2 * L, FL - 2 * L)], store_sem.at[0])
    rest.start()

    for half in range(2):
        lanes = slice(half * HALF, (half + 1) * HALF)
        base = half * HROWS
        levels = slice(half * ZROWS, half * ZROWS + CZ)
        arrived = recv.at[pl.ds(half * N // 2, N // 2)]
        pltpu.make_async_copy(arrived, arrived, fwd_recv.at[half]).wait()
        columns = recv[half * N // 2 : (half + 1) * N // 2].reshape(HALF, 2 * L)
        both = lax.dot_general(
            weights[...], columns, (((1,), (1,)), ((), ())), precision=HIGHEST, preferred_element_type=jnp.float32
        )
        forcing = both[0:CZ]
        courant = max_courant * jax.nn.sigmoid(both[L : L + CZ])
        keep = 1.0 - courant
        nudge = relax_rate * (forcing - mean[levels, :])
        a1[0:CZ, :] = keep * rl[levels, :]
        b1[0:CZ, :] = courant * rl[levels, :]
        d1[0:CZ, :] = nudge * rl[levels, :]
        a2[0:CZ, :] = keep * ru[levels, :]
        b2[0:CZ, :] = courant * ru[levels, :]

        def row(ref, level, first=0):
            return ref[pl.ds(first + level, 1), :]

        def behind(values):
            last = pltpu.roll(values[CX - 8 : CX], 1, 0)
            return jnp.concatenate([last, values[0 : CX - 8]], axis=0)

        def up_sweep(level, carry):
            spot = pl.ds(pl.multiple_of(base + level * CX, 8), CX)
            values = field[spot, :]
            carry = (
                values * row(a1, level)
                + behind(values) * row(b1, level)
                + (row(d1, level) + row(cl, level, half * ZROWS) * carry)
            )
            field[spot, :] = carry
            return carry

        def down_sweep(i, carry):
            level = CZ - 1 - i
            solved, partial = carry
            spot = pl.ds(pl.multiple_of(base + level * CX, 8), CX)
            solved = field[spot, :] + row(el, level, half * ZROWS) * solved
            partial = solved * row(a2, level) + behind(solved) * row(b2, level) + row(cu, level, half * ZROWS) * partial
            field[spot, :] = partial
            return solved, partial

        def last_sweep(level, carry):
            spot = pl.ds(pl.multiple_of(base + level * CX, 8), CX)
            carry = field[spot, :] + row(eu, level, half * ZROWS) * carry
            field[spot, :] = carry
            eight = carry.reshape(8, 8, HALF)
            here = pl.ds(pl.multiple_of(level * 8, 8), 8)
            part[here, :] = jnp.sum(eight, axis=0)
            partsq[here, :] = jnp.sum(eight * eight, axis=0)
            return carry

        none = jnp.zeros((CX, HALF), jnp.float32)
        lax.fori_loop(0, CZ, up_sweep, none)
        lax.fori_loop(0, CZ, down_sweep, (none, none))
        lax.fori_loop(0, CZ, last_sweep, none)

        def level_sums(ref):
            blocks = []
            for block in range(ZROWS // 8):
                rows = min(8, CZ - 8 * block)
                total = ref[pl.ds(block * 64, rows, stride=8), :]
                for s in range(1, 8):
                    total = total + ref[pl.ds(block * 64 + s, rows, stride=8), :]
                blocks.append(total)
            return jnp.concatenate(blocks, axis=0) * (1.0 / CX)

        mean_after = level_sums(part)
        spread_after = level_sums(partsq) - mean_after * mean_after
        delta[0:CZ, lanes] = mean_after - mean[levels, :]
        delta[L : L + CZ, lanes] = spread_after - spread[levels, :]
        tend = lax.dot_general(
            delta[:, lanes], weights[...], (((0,), (0,)), ((), ())), precision=HIGHEST, preferred_element_type=jnp.float32
        )
        reply[half * N // 2 : (half + 1) * N // 2] = tend.reshape(N // 2, 2, 2 * L)

        def back(i, carry):
            ring, plane = i // 4, lax.rem(i, 4)
            peer = index_of(
                2 * half + lax.rem(x + plane // NC + 1, 2),
                around(z + NZ // 2 + far(ring), NZ),
                lax.rem(core + 1 - lax.rem(plane, NC), NC),
            )

            @pl.when(peer != me)
            def _():
                pltpu.make_async_remote_copy(
                    reply.at[peer], ret.at[me], rep_send, rep_recv, device_id=(peer, strip), device_id_type=MESH
                ).start()

            return carry

        lax.fori_loop(0, N // 2, back, 0)

        @pl.when(x // 2 == half)
        def _():
            pltpu.make_async_copy(reply.at[me], ret.at[me], rep_recv).start()

    def store(column, carry):
        spot = lax.rem(column, 8) * 8 + column // 8
        for half in range(2):
            blocks = []
            for block in range(ZROWS // 8):
                rows = min(8, CZ - 8 * block)
                blocks.append(field[pl.ds(half * HROWS + block * 8 * CX + spot, rows, stride=CX), :])
            start = pl.multiple_of(column * SLOTS + half * HALF, HALF)
            crm[:, pl.ds(start, HALF)] = jnp.concatenate(blocks, axis=0).astype(jnp.bfloat16)
        return carry

    crm_stores = []
    for i in range(pieces):
        lax.fori_loop(i * CX // pieces, (i + 1) * CX // pieces, store, 0)
        crm_stores.append(
            pltpu.make_async_copy(
                crm.at[:, pl.ds(i * width, width)], out_hbm.at[0, 0, :, pl.ds(i * width, width)], crm_out_sem.at[i]
            )
        )
        crm_stores[-1].start()

    pltpu.make_async_copy(ret, ret, rep_recv).wait()
    both = lax.dot_general(
        picks, split(ret[...].reshape(SLOTS, 2 * L)), (((0,), (0,)), ((), ())), preferred_element_type=jnp.float32
    )
    moved[:, 0 : 2 * L] = moved[:, 0 : 2 * L] + (both[:, 0 : 2 * L] + both[:, 2 * L :])
    first = pltpu.make_async_copy(moved.at[:, pl.ds(0, 2 * L)], new_hbm.at[0, :, pl.ds(0, 2 * L)], store_sem.at[1])
    first.start()
    sent = send.at[pl.ds(0, N - 1)]
    pltpu.make_async_copy(sent, sent, fwd_send).wait()
    pltpu.make_async_copy(sent, sent, rep_send).wait()
    for piece in crm_stores:
        piece.wait()
    rest.wait()
    first.wait()


def shards(state, owners, orient, crm_state, active_levels, vertical_map, diffusion):
    f32 = jnp.float32
    anywhere = pl.BlockSpec(memory_space=pl.ANY)
    level_rows = pltpu.VMEM((2 * ZROWS, HALF), f32)
    half_rows = pltpu.VMEM((ZROWS, HALF), f32)
    chunks = pltpu.VMEM((N, 2, 2 * L), f32)
    dma = pltpu.SemaphoreType.DMA
    return pl.pallas_call(
        kernel,
        out_shape=(
            jax.ShapeDtypeStruct(state.shape, f32),
            jax.ShapeDtypeStruct(crm_state.shape, jnp.bfloat16),
        ),
        in_specs=[anywhere] * 7,
        out_specs=(anywhere, anywhere),
        scratch_shapes=[
            pltpu.VMEM((2 * TW + CPD, FL), f32),
            pltpu.VMEM((2, TW, FL), f32),
            pltpu.VMEM((1, CPD), jnp.int32),
            pltpu.VMEM((1, SLOTS), jnp.int32),
            pltpu.VMEM((CZ, L), f32),
            pltpu.SMEM((1, 2), jnp.int32),
            pltpu.SMEM((1, CZ - 1), f32),
            pltpu.VMEM((CZ, CX * SLOTS), jnp.bfloat16),
            pltpu.VMEM((2 * HROWS, HALF), f32),
            *[level_rows] * 6,
            *[half_rows] * 5,
            *[level_rows] * 2,
            pltpu.VMEM((ZROWS * 8, HALF), f32),
            pltpu.VMEM((ZROWS * 8, HALF), f32),
            pltpu.VMEM((CPD, CPD), f32),
            pltpu.VMEM((CPD, SLOTS), f32),
            pltpu.VMEM((CPD, FL), f32),
            chunks,
            chunks,
            chunks,
            chunks,
            pltpu.SemaphoreType.REGULAR,
            dma((6,)),
            dma((4,)),
            dma((2,)),
            dma((2,)),
            dma,
            dma((2,)),
            dma,
            dma,
            dma((2,)),
            dma((4,)),
        ],
        compiler_params=pltpu.CompilerParams(collective_id=0, has_side_effects=True, vmem_limit_bytes=48 << 20),
    )(
        state,
        owners.reshape(1, CPD),
        orient.reshape(1, 2),
        crm_state,
        active_levels.reshape(1, SLOTS),
        vertical_map,
        diffusion.reshape(1, CZ - 1),
    )


def solution(mesh):
    in_specs = (
        P("edge", "cols", None),
        P("edge", "cols", None),
        P("edge", "cols", None),
        P("edge", "cols", None, None),
        P("edge", "cols", None),
        P(),
        P(),
    )
    out_specs = (P("edge", "cols", None), P("edge", "cols", None, None))
    return jax.shard_map(shards, mesh=mesh, in_specs=in_specs, out_specs=out_specs, check_vma=False)
```

```python
import functools

import jax
import jax.numpy as jnp
from jax import lax
from jax.experimental import pallas as pl
from jax.experimental.pallas import tpu as pltpu
from jax.sharding import PartitionSpec as P

MESH = pl.DeviceIdType.MESH

L = 64
CX = 64
CZ = 58
TW = 8
CPD = 128
FL = 512
SLOTS = 256
HALF = 128
N = 128
NX, NZ, NC, NE = 4, 16, 2, 4
ZROWS = 64
HROWS = ZROWS * CX

kappa_edge = 0.25
max_courant = 0.9
relax_rate = 0.5

HIGHEST = lax.Precision.HIGHEST


def index_of(x, z, core):
    return (x * NZ + z) * NC + core


def around(value, count):
    return lax.rem(value + count, count)


def split(values):
    high = values.astype(jnp.bfloat16)
    low = (values - high.astype(jnp.float32)).astype(jnp.bfloat16)
    return jnp.concatenate([high, low], axis=1)


def kernel(
    state_hbm, owners_hbm, orient_hbm, crm_hbm, active_hbm, vmap_hbm, diff_hbm,
    new, out,
    tile, ghosts, owner, active, vmap, orient, diff, crm, field,
    rl, cl, el, ru, cu, eu, a1, b1, d1, a2, b2, mean, spread, part, partsq,
    weights, delta, send, recv, reply, ret,
    ready, load_sem, crm_sem, halo_send, halo_recv, fwd_send, fwd_recv, rep_send, rep_recv,
):
    me = lax.axis_index("cols")
    strip = lax.axis_index("edge")
    x = me // (NZ * NC)
    z = lax.rem(me // NC, NZ)
    core = lax.rem(me, NC)
    above = around(strip + 1, NE)
    below = around(strip - 1, NE)

    barrier = pltpu.get_barrier_semaphore()

    def greet(column, row):
        pl.semaphore_signal(barrier, inc=1, device_id=(column, row), device_id_type=MESH)

    def greet_ring(i, carry):
        greet(index_of(x, around(z + i, NZ), core), strip)
        return carry

    def plane_peer(i):
        i = i + core + NC * x
        return index_of(lax.rem(i // NC, NX), z, lax.rem(i, NC))

    def greet_plane(i, carry):
        greet(plane_peer(i), strip)
        return carry

    lax.fori_loop(1, NZ, greet_ring, 0)
    lax.fori_loop(1, NX * NC, greet_plane, 0)
    greet(me, above)
    greet(me, below)

    loads = [
        pltpu.make_async_copy(state_hbm.at[0], tile.at[pl.ds(TW, CPD)], load_sem.at[0]),
        pltpu.make_async_copy(owners_hbm, owner, load_sem.at[1]),
        pltpu.make_async_copy(active_hbm, active, load_sem.at[2]),
        pltpu.make_async_copy(vmap_hbm, vmap, load_sem.at[3]),
        pltpu.make_async_copy(orient_hbm, orient, load_sem.at[4]),
        pltpu.make_async_copy(diff_hbm, diff, load_sem.at[5]),
    ]
    for load in loads:
        load.start()
    pieces = 4
    width = CX * SLOTS // pieces
    crm_loads = [
        pltpu.make_async_copy(
            crm_hbm.at[0, 0, :, pl.ds(i * width, width)], crm.at[:, pl.ds(i * width, width)], crm_sem.at[i]
        )
        for i in range(pieces)
    ]
    for load in crm_loads:
        load.start()
    for load in loads:
        load.wait()

    group = owner[...]
    line = lax.broadcasted_iota(jnp.int32, (CPD, CPD), 0)
    along = lax.broadcasted_iota(jnp.int32, (CPD, CPD), 1)
    named = jnp.where(line == group, 1.0, 0.0)
    earlier = jnp.where(line < along, 1.0, 0.0)
    before = jnp.dot(named.astype(jnp.bfloat16), earlier.astype(jnp.bfloat16), preferred_element_type=jnp.float32)
    rank = jnp.sum(named * before, axis=0, keepdims=True)
    slot = group * 2 + rank.astype(jnp.int32)
    picks = jnp.where(lax.broadcasted_iota(jnp.int32, (SLOTS, CPD), 0) == slot, 1.0, 0.0).astype(jnp.bfloat16)

    pl.semaphore_wait(barrier, NZ - 1 + NX * NC - 1 + 2)

    def announce(i, carry):
        pl.semaphore_signal(ready, inc=1, device_id=(plane_peer(i), strip), device_id_type=MESH)
        return carry

    upward = pltpu.make_async_remote_copy(
        state_hbm.at[0, pl.ds(CPD - TW, TW)], ghosts.at[0], halo_send.at[0], halo_recv.at[0],
        device_id=(me, above), device_id_type=MESH,
    )
    downward = pltpu.make_async_remote_copy(
        state_hbm.at[0, pl.ds(0, TW)], ghosts.at[1], halo_send.at[1], halo_recv.at[1],
        device_id=(me, below), device_id_type=MESH,
    )
    upward.start()
    downward.start()
    lax.fori_loop(1, NX * NC, announce, 0)
    upward.wait()
    downward.wait()
    for side in range(2):
        flip = orient[0, side] == 1
        for w in range(TW):
            row = side * (TW + CPD) + w
            tile[row : row + 1, :] = jnp.where(flip, ghosts[side, TW - 1 - w : TW - w, :], ghosts[side, w : w + 1, :])

    def step(lanes):
        here = tile[TW : TW + CPD, lanes]
        return here + kappa_edge * ((tile[2 * TW : 2 * TW + CPD, lanes] + tile[0:CPD, lanes]) - 2.0 * here)

    used = step(slice(0, 2 * L))
    new[0, :, 0 : 2 * L] = used
    both = jnp.dot(picks, split(used), preferred_element_type=jnp.float32)
    send[...] = (both[:, 0 : 2 * L] + both[:, 2 * L :]).reshape(N, 2, 2 * L)
    pl.semaphore_wait(ready, NX * NC - 1)

    far = z + NZ // 2

    def rings(send_ring):
        send_ring(lax.rem(far, NZ))

        def pair(i, carry):
            send_ring(lax.rem(far + i, NZ))
            send_ring(lax.rem(far - i, NZ))
            return carry

        lax.fori_loop(1, NZ // 2, pair, 0)

    others = [
        (lax.rem(x + dx, NX) * (NZ * NC) + lax.rem(core + dc, NC)) for dx in (2, 1, 3, 0) for dc in (1, 0)
    ]
    arrival = fwd_recv.at[lax.div(x, 2)]

    def forward(peers, level):
        for plane in peers:
            peer = plane + level * NC
            pltpu.make_async_remote_copy(
                send.at[peer], recv.at[me], fwd_send, arrival, device_id=(peer, strip), device_id_type=MESH
            ).start()

    rings(functools.partial(forward, others))
    forward(others[:-1], z)
    pltpu.make_async_copy(send.at[me], recv.at[me], arrival).start()

    new[0, :, 2 * L :] = step(slice(2 * L, FL))

    count = active[...]

    def put(ref, level, values):
        for half in range(2):
            ref[pl.ds(half * ZROWS + level, 1), :] = values[:, half * HALF : (half + 1) * HALF]

    def factor(i, carry):
        lower_e, upper_e, k_before, k_after = carry
        level = i
        k_here = jnp.where(level + 1 < count, diff[0, jnp.minimum(level, CZ - 2)], 0.0)
        k_here = jnp.where(level < CZ - 1, k_here, 0.0)
        inv = 1.0 / (1.0 + k_before + k_here - k_before * lower_e)
        lower_e = k_here * inv
        put(rl, level, inv)
        put(cl, level, k_before * inv)
        put(el, level, lower_e)
        top = CZ - 1 - i
        k_under = jnp.where(top < count, diff[0, jnp.maximum(top - 1, 0)], 0.0)
        k_under = jnp.where(top > 0, k_under, 0.0)
        inv_u = 1.0 / (1.0 + k_after + k_under - k_after * upper_e)
        upper_e = k_under * inv_u
        put(ru, top, inv_u)
        put(cu, top, k_after * inv_u)
        put(eu, top, upper_e)
        return lower_e, upper_e, k_here, k_under

    zero_row = jnp.zeros((1, SLOTS), jnp.float32)
    lax.fori_loop(0, CZ, factor, (zero_row, zero_row, zero_row, zero_row))

    weights[...] = jnp.zeros((CPD, CPD), jnp.float32)
    weights[0:CZ, 0:L] = vmap[...]
    weights[L : L + CZ, L : 2 * L] = vmap[...]
    delta[...] = jnp.zeros((CPD, SLOTS), jnp.float32)

    sums = tuple(jnp.zeros((CZ, HALF), jnp.float32) for _ in range(4))

    def relayout(column, carry):
        carry = list(carry)
        spot = lax.rem(column, 8) * 8 + column // 8
        for half in range(2):
            start = pl.multiple_of(column * SLOTS + half * HALF, HALF)
            values = crm[:, pl.ds(start, HALF)].astype(jnp.float32)
            carry[half] = carry[half] + values
            carry[2 + half] = carry[2 + half] + values * values
            for block in range(ZROWS // 8):
                rows = min(8, CZ - 8 * block)
                field[pl.ds(half * HROWS + block * 8 * CX + spot, rows, stride=CX), :] = values[8 * block : 8 * block + rows]
        return tuple(carry)

    for i in range(pieces):
        crm_loads[i].wait()
        sums = lax.fori_loop(i * CX // pieces, (i + 1) * CX // pieces, relayout, sums)
    for half in range(2):
        levels = slice(half * ZROWS, half * ZROWS + CZ)
        average = sums[half] * (1.0 / CX)
        mean[levels, :] = average
        spread[levels, :] = sums[2 + half] * (1.0 / CX) - average * average

    for half in range(2):
        lanes = slice(half * HALF, (half + 1) * HALF)
        base = half * HROWS
        levels = slice(half * ZROWS, half * ZROWS + CZ)
        arrived = recv.at[pl.ds(half * N // 2, N // 2)]
        pltpu.make_async_copy(arrived, arrived, fwd_recv.at[half]).wait()
        columns = recv[half * N // 2 : (half + 1) * N // 2].reshape(HALF, 2 * L)
        both = lax.dot_general(
            weights[...], columns, (((1,), (1,)), ((), ())), precision=HIGHEST, preferred_element_type=jnp.float32
        )
        forcing = both[0:CZ]
        courant = max_courant * jax.nn.sigmoid(both[L : L + CZ])
        keep = 1.0 - courant
        nudge = relax_rate * (forcing - mean[levels, :])
        a1[0:CZ, :] = keep * rl[levels, :]
        b1[0:CZ, :] = courant * rl[levels, :]
        d1[0:CZ, :] = nudge * rl[levels, :]
        a2[0:CZ, :] = keep * ru[levels, :]
        b2[0:CZ, :] = courant * ru[levels, :]

        def row(ref, level, first=0):
            return ref[pl.ds(first + level, 1), :]

        def behind(values):
            last = pltpu.roll(values[CX - 8 : CX], 1, 0)
            return jnp.concatenate([last, values[0 : CX - 8]], axis=0)

        def up_sweep(level, carry):
            spot = pl.ds(pl.multiple_of(base + level * CX, 8), CX)
            values = field[spot, :]
            carry = (
                values * row(a1, level)
                + behind(values) * row(b1, level)
                + (row(d1, level) + row(cl, level, half * ZROWS) * carry)
            )
            field[spot, :] = carry
            return carry

        def down_sweep(i, carry):
            level = CZ - 1 - i
            solved, partial = carry
            spot = pl.ds(pl.multiple_of(base + level * CX, 8), CX)
            solved = field[spot, :] + row(el, level, half * ZROWS) * solved
            partial = solved * row(a2, level) + behind(solved) * row(b2, level) + row(cu, level, half * ZROWS) * partial
            field[spot, :] = partial
            return solved, partial

        def last_sweep(level, carry):
            spot = pl.ds(pl.multiple_of(base + level * CX, 8), CX)
            carry = field[spot, :] + row(eu, level, half * ZROWS) * carry
            field[spot, :] = carry
            eight = carry.reshape(8, 8, HALF)
            here = pl.ds(pl.multiple_of(level * 8, 8), 8)
            part[here, :] = jnp.sum(eight, axis=0)
            partsq[here, :] = jnp.sum(eight * eight, axis=0)
            return carry

        none = jnp.zeros((CX, HALF), jnp.float32)
        lax.fori_loop(0, CZ, up_sweep, none)
        lax.fori_loop(0, CZ, down_sweep, (none, none))
        lax.fori_loop(0, CZ, last_sweep, none)

        def level_sums(ref):
            blocks = []
            for block in range(ZROWS // 8):
                rows = min(8, CZ - 8 * block)
                total = ref[pl.ds(block * 64, rows, stride=8), :]
                for s in range(1, 8):
                    total = total + ref[pl.ds(block * 64 + s, rows, stride=8), :]
                blocks.append(total)
            return jnp.concatenate(blocks, axis=0) * (1.0 / CX)

        mean_after = level_sums(part)
        spread_after = level_sums(partsq) - mean_after * mean_after
        delta[0:CZ, lanes] = mean_after - mean[levels, :]
        delta[L : L + CZ, lanes] = spread_after - spread[levels, :]
        tend = lax.dot_general(
            delta[:, lanes], weights[...], (((0,), (0,)), ((), ())), precision=HIGHEST, preferred_element_type=jnp.float32
        )
        reply[half * N // 2 : (half + 1) * N // 2] = tend.reshape(N // 2, 2, 2 * L)

        targets = [xt * (NZ * NC) + ct for xt in (2 * half, 2 * half + 1) for ct in range(NC)]

        def back(peers, level):
            for plane in peers:
                peer = plane + level * NC
                pltpu.make_async_remote_copy(
                    reply.at[peer], ret.at[me], rep_send, rep_recv, device_id=(peer, strip), device_id_type=MESH
                ).start()

        rings(functools.partial(back, targets))
        for plane in targets:

            @pl.when(plane + z * NC != me)
            def _(plane=plane):
                back([plane], z)

        @pl.when(x // 2 == half)
        def _():
            pltpu.make_async_copy(reply.at[me], ret.at[me], rep_recv).start()

    def store(column, carry):
        spot = lax.rem(column, 8) * 8 + column // 8
        for half in range(2):
            blocks = []
            for block in range(ZROWS // 8):
                rows = min(8, CZ - 8 * block)
                blocks.append(field[pl.ds(half * HROWS + block * 8 * CX + spot, rows, stride=CX), :])
            start = pl.multiple_of(column * SLOTS + half * HALF, HALF)
            out[0, 0, :, pl.ds(start, HALF)] = jnp.concatenate(blocks, axis=0).astype(jnp.bfloat16)
        return carry

    lax.fori_loop(0, CX, store, 0)

    pltpu.make_async_copy(ret, ret, rep_recv).wait()
    both = lax.dot_general(
        picks, split(ret[...].reshape(SLOTS, 2 * L)), (((0,), (0,)), ((), ())), preferred_element_type=jnp.float32
    )
    new[0, :, 0 : 2 * L] = new[0, :, 0 : 2 * L] + (both[:, 0 : 2 * L] + both[:, 2 * L :])
    sent = send.at[pl.ds(0, N - 1)]
    pltpu.make_async_copy(sent, sent, fwd_send).wait()
    pltpu.make_async_copy(sent, sent, rep_send).wait()

def ship(new, out, new_hbm, out_hbm, sems):
    pieces = 8
    width = CX * SLOTS // pieces
    copies = [pltpu.make_async_copy(new, new_hbm, sems.at[pieces])]
    for i in range(pieces):
        lanes = pl.ds(i * width, width)
        copies.append(pltpu.make_async_copy(out.at[0, 0, :, lanes], out_hbm.at[0, 0, :, lanes], sems.at[i]))
    for copy in copies:
        copy.start()
    for copy in copies:
        copy.wait()


def shards(state, owners, orient, crm_state, active_levels, vertical_map, diffusion):
    f32 = jnp.float32
    anywhere = pl.BlockSpec(memory_space=pl.ANY)
    level_rows = pltpu.VMEM((2 * ZROWS, HALF), f32)
    half_rows = pltpu.VMEM((ZROWS, HALF), f32)
    chunks = pltpu.VMEM((N, 2, 2 * L), f32)
    dma = pltpu.SemaphoreType.DMA
    new, out = pl.pallas_call(
        kernel,
        out_shape=(
            pltpu.VMEM(state.shape, f32),
            pltpu.VMEM(crm_state.shape, jnp.bfloat16),
        ),
        in_specs=[anywhere] * 7,
        out_specs=(pl.BlockSpec(memory_space=pltpu.VMEM),) * 2,
        scratch_shapes=[
            pltpu.VMEM((2 * TW + CPD, FL), f32),
            pltpu.VMEM((2, TW, FL), f32),
            pltpu.VMEM((1, CPD), jnp.int32),
            pltpu.VMEM((1, SLOTS), jnp.int32),
            pltpu.VMEM((CZ, L), f32),
            pltpu.SMEM((1, 2), jnp.int32),
            pltpu.SMEM((1, CZ - 1), f32),
            pltpu.VMEM((CZ, CX * SLOTS), jnp.bfloat16),
            pltpu.VMEM((2 * HROWS, HALF), f32),
            *[level_rows] * 6,
            *[half_rows] * 5,
            *[level_rows] * 2,
            pltpu.VMEM((ZROWS * 8, HALF), f32),
            pltpu.VMEM((ZROWS * 8, HALF), f32),
            pltpu.VMEM((CPD, CPD), f32),
            pltpu.VMEM((CPD, SLOTS), f32),
            chunks,
            chunks,
            chunks,
            chunks,
            pltpu.SemaphoreType.REGULAR,
            dma((6,)),
            dma((4,)),
            dma((2,)),
            dma((2,)),
            dma,
            dma((2,)),
            dma,
            dma,
        ],
        compiler_params=pltpu.CompilerParams(collective_id=0, has_side_effects=True, vmem_limit_bytes=56 << 20),
    )(
        state,
        owners.reshape(1, CPD),
        orient.reshape(1, 2),
        crm_state,
        active_levels.reshape(1, SLOTS),
        vertical_map,
        diffusion.reshape(1, CZ - 1),
    )
    return pl.pallas_call(
        ship,
        out_shape=(
            pltpu.HBM(state.shape, f32),
            pltpu.HBM(crm_state.shape, jnp.bfloat16),
        ),
        in_specs=[anywhere] * 2,
        out_specs=(pl.BlockSpec(memory_space=pltpu.HBM),) * 2,
        scratch_shapes=[dma((9,))],
        compiler_params=pltpu.CompilerParams(vmem_limit_bytes=8 << 20),
    )(new, out)


def solution(mesh):
    in_specs = (
        P("edge", "cols", None),
        P("edge", "cols", None),
        P("edge", "cols", None),
        P("edge", "cols", None, None),
        P("edge", "cols", None),
        P(),
        P(),
    )
    out_specs = (P("edge", "cols", None), P("edge", "cols", None, None))
    return jax.shard_map(shards, mesh=mesh, in_specs=in_specs, out_specs=out_specs, check_vma=False)
```

```python
import functools

import jax
import jax.numpy as jnp
from jax import lax
from jax.experimental import pallas as pl
from jax.experimental.pallas import tpu as pltpu
from jax.sharding import PartitionSpec as P

MESH = pl.DeviceIdType.MESH

L = 64
CX = 64
CZ = 58
TW = 8
CPD = 128
FL = 512
SLOTS = 256
HALF = 128
N = 128
NX, NZ, NC, NE = 4, 16, 2, 4
ZROWS = 64
HROWS = ZROWS * CX

kappa_edge = 0.25
max_courant = 0.9
relax_rate = 0.5

UNROLL = 29


def index_of(x, z, core):
    return (x * NZ + z) * NC + core


def around(value, count):
    return lax.rem(value + count, count)


def split(values):
    high = values.astype(jnp.bfloat16)
    low = (values - high.astype(jnp.float32)).astype(jnp.bfloat16)
    return jnp.concatenate([high, low], axis=1)


def product(left, right, left_dim, right_dim):
    def parts(values):
        high = values.astype(jnp.bfloat16)
        return high, (values - high.astype(jnp.float32)).astype(jnp.bfloat16)

    def dot(a, b):
        return lax.dot_general(a, b, (((left_dim,), (right_dim,)), ((), ())), preferred_element_type=jnp.float32)

    left_high, left_low = parts(left)
    right_high, right_low = parts(right)
    return dot(left_high, right_high) + (dot(left_high, right_low) + dot(left_low, right_high))


def kernel(
    state_hbm, owners_hbm, orient_hbm, crm_hbm, active_hbm, vmap_hbm, diff_hbm,
    new, out,
    tile, ghosts, owner, active, vmap, orient, diff, crm, field,
    rl, cl, el, ru, cu, eu, a1, b1, d1, a2, b2, mean, spread, part, partsq,
    weights, delta, send, recv, reply, ret,
    ready, load_sem, crm_sem, halo_send, halo_recv, fwd_send, fwd_recv, rep_send, rep_recv,
):
    me = lax.axis_index("cols")
    strip = lax.axis_index("edge")
    x = me // (NZ * NC)
    z = lax.rem(me // NC, NZ)
    core = lax.rem(me, NC)
    above = around(strip + 1, NE)
    below = around(strip - 1, NE)

    barrier = pltpu.get_barrier_semaphore()

    def greet(column, row):
        pl.semaphore_signal(barrier, inc=1, device_id=(column, row), device_id_type=MESH)

    far = z + NZ // 2

    def ring(level):
        greet(index_of(x, lax.rem(level, NZ), core), strip)

    ring(far)

    def greet_pair(i, carry):
        ring(far - i)
        ring(far + i)
        return carry

    lax.fori_loop(1, NZ // 2, greet_pair, 0)

    planes = [
        (lax.rem(x + dx, NX) * (NZ * NC) + lax.rem(core + dc, NC)) for dx in (2, 1, 3, 0) for dc in (1, 0)
    ]
    for plane in planes[:-1]:
        greet(plane + z * NC, strip)
    greet(me, above)
    greet(me, below)

    loads = [
        pltpu.make_async_copy(state_hbm.at[0], tile.at[pl.ds(TW, CPD)], load_sem.at[0]),
        pltpu.make_async_copy(owners_hbm, owner, load_sem.at[1]),
        pltpu.make_async_copy(active_hbm, active, load_sem.at[2]),
        pltpu.make_async_copy(vmap_hbm, vmap, load_sem.at[3]),
        pltpu.make_async_copy(orient_hbm, orient, load_sem.at[4]),
        pltpu.make_async_copy(diff_hbm, diff, load_sem.at[5]),
    ]
    for load in loads:
        load.start()
    pieces = 4
    width = CX * SLOTS // pieces
    crm_loads = [
        pltpu.make_async_copy(
            crm_hbm.at[0, 0, :, pl.ds(i * width, width)], crm.at[:, pl.ds(i * width, width)], crm_sem.at[i]
        )
        for i in range(pieces)
    ]
    for load in crm_loads:
        load.start()
    for load in loads:
        load.wait()

    group = owner[...]
    line = lax.broadcasted_iota(jnp.int32, (CPD, CPD), 0)
    along = lax.broadcasted_iota(jnp.int32, (CPD, CPD), 1)
    named = jnp.where(line == group, 1.0, 0.0)
    earlier = jnp.where(line < along, 1.0, 0.0)
    before = jnp.dot(named.astype(jnp.bfloat16), earlier.astype(jnp.bfloat16), preferred_element_type=jnp.float32)
    rank = jnp.sum(named * before, axis=0, keepdims=True)
    slot = group * 2 + rank.astype(jnp.int32)
    picks = jnp.where(lax.broadcasted_iota(jnp.int32, (SLOTS, CPD), 0) == slot, 1.0, 0.0).astype(jnp.bfloat16)

    pl.semaphore_wait(barrier, NZ - 1 + NX * NC - 1 + 2)

    parts = (slice(0, 2 * L), slice(2 * L, FL))
    trades = []
    for i, lanes in enumerate(parts):
        for side, (first, row) in enumerate(((CPD, above), (TW, below))):
            trades.append(
                pltpu.make_async_remote_copy(
                    tile.at[pl.ds(first, TW), lanes], ghosts.at[side, :, lanes],
                    halo_send.at[2 * i + side], halo_recv.at[2 * i + side],
                    device_id=(me, row), device_id_type=MESH,
                )
            )
            trades[-1].start()
    for plane in planes[:-1]:
        pl.semaphore_signal(ready, inc=1, device_id=(plane + z * NC, strip), device_id_type=MESH)

    def settle(i):
        lanes = parts[i]
        for side in range(2):
            trades[2 * i + side].wait()
            flip = orient[0, side] == 1
            for w in range(TW):
                row = side * (TW + CPD) + w
                tile[row : row + 1, lanes] = jnp.where(
                    flip, ghosts[side, TW - 1 - w : TW - w, lanes], ghosts[side, w : w + 1, lanes]
                )

    settle(0)

    def step(lanes):
        here = tile[TW : TW + CPD, lanes]
        return here + kappa_edge * ((tile[2 * TW : 2 * TW + CPD, lanes] + tile[0:CPD, lanes]) - 2.0 * here)

    used = step(slice(0, 2 * L))
    new[0, :, 0 : 2 * L] = used
    both = jnp.dot(picks, split(used), preferred_element_type=jnp.float32)
    send[...] = (both[:, 0 : 2 * L] + both[:, 2 * L :]).reshape(N, 2, 2 * L)
    pl.semaphore_wait(ready, NX * NC - 1)

    def rings(send_ring):
        send_ring(lax.rem(far, NZ))

        def pair(i, carry):
            send_ring(lax.rem(far - i, NZ))
            send_ring(lax.rem(far + i, NZ))
            return carry

        lax.fori_loop(1, NZ // 2, pair, 0)

    arrival = fwd_recv.at[lax.div(x, 2)]

    def forward(peers, level):
        for plane in peers:
            peer = plane + level * NC
            pltpu.make_async_remote_copy(
                send.at[peer], recv.at[me], fwd_send, arrival, device_id=(peer, strip), device_id_type=MESH
            ).start()

    def forward_all():
        rings(functools.partial(forward, planes))
        forward(planes[:-1], z)
        pltpu.make_async_copy(send.at[me], recv.at[me], arrival).start()

    forward_all()

    sums = tuple(jnp.zeros((CZ, HALF), jnp.float32) for _ in range(4))

    def relayout(column, carry):
        carry = list(carry)
        spot = lax.rem(column, 8) * 8 + column // 8
        for half in range(2):
            start = pl.multiple_of(column * SLOTS + half * HALF, HALF)
            values = crm[:, pl.ds(start, HALF)].astype(jnp.float32)
            carry[half] = carry[half] + values
            carry[2 + half] = carry[2 + half] + values * values
            for block in range(ZROWS // 8):
                rows = min(8, CZ - 8 * block)
                field[pl.ds(half * HROWS + block * 8 * CX + spot, rows, stride=CX), :] = values[8 * block : 8 * block + rows]
        return tuple(carry)

    for i in range(pieces):
        crm_loads[i].wait()
        sums = lax.fori_loop(i * CX // pieces, (i + 1) * CX // pieces, relayout, sums)
    for half in range(2):
        levels = slice(half * ZROWS, half * ZROWS + CZ)
        average = sums[half] * (1.0 / CX)
        mean[levels, :] = average
        spread[levels, :] = sums[2 + half] * (1.0 / CX) - average * average

    settle(1)
    new[0, :, 2 * L :] = step(slice(2 * L, FL))

    count = active[...]

    def put(ref, level, values):
        for half in range(2):
            ref[pl.ds(half * ZROWS + level, 1), :] = values[:, half * HALF : (half + 1) * HALF]

    def factor(i, carry):
        lower_e, upper_e, k_before, k_after = carry
        level = i
        k_here = jnp.where(level + 1 < count, diff[0, jnp.minimum(level, CZ - 2)], 0.0)
        k_here = jnp.where(level < CZ - 1, k_here, 0.0)
        inv = 1.0 / (1.0 + k_before + k_here - k_before * lower_e)
        lower_e = k_here * inv
        put(rl, level, inv)
        put(cl, level, k_before * inv)
        put(el, level, lower_e)
        top = CZ - 1 - i
        k_under = jnp.where(top < count, diff[0, jnp.maximum(top - 1, 0)], 0.0)
        k_under = jnp.where(top > 0, k_under, 0.0)
        inv_u = 1.0 / (1.0 + k_after + k_under - k_after * upper_e)
        upper_e = k_under * inv_u
        put(ru, top, inv_u)
        put(cu, top, k_after * inv_u)
        put(eu, top, upper_e)
        return lower_e, upper_e, k_here, k_under

    zero_row = jnp.zeros((1, SLOTS), jnp.float32)
    lax.fori_loop(0, CZ, factor, (zero_row, zero_row, zero_row, zero_row))

    weights[...] = jnp.zeros((CPD, CPD), jnp.float32)
    weights[0:CZ, 0:L] = vmap[...]
    weights[L : L + CZ, L : 2 * L] = vmap[...]
    delta[...] = jnp.zeros((CPD, SLOTS), jnp.float32)

    for half in range(2):
        lanes = slice(half * HALF, (half + 1) * HALF)
        base = half * HROWS
        levels = slice(half * ZROWS, half * ZROWS + CZ)
        arrived = recv.at[pl.ds(half * N // 2, N // 2)]
        pltpu.make_async_copy(arrived, arrived, fwd_recv.at[half]).wait()
        columns = recv[half * N // 2 : (half + 1) * N // 2].reshape(HALF, 2 * L)
        both = product(weights[...], columns, 1, 1)
        forcing = both[0:CZ]
        courant = max_courant * jax.nn.sigmoid(both[L : L + CZ])
        keep = 1.0 - courant
        nudge = relax_rate * (forcing - mean[levels, :])
        a1[0:CZ, :] = keep * rl[levels, :]
        b1[0:CZ, :] = courant * rl[levels, :]
        d1[0:CZ, :] = nudge * rl[levels, :]
        a2[0:CZ, :] = keep * ru[levels, :]
        b2[0:CZ, :] = courant * ru[levels, :]

        def row(ref, level, first=0):
            return ref[pl.ds(first + level, 1), :]

        def behind(values):
            last = pltpu.roll(values[CX - 8 : CX], 1, 0)
            return jnp.concatenate([last, values[0 : CX - 8]], axis=0)

        def up_sweep(level, carry):
            spot = pl.ds(pl.multiple_of(base + level * CX, 8), CX)
            values = field[spot, :]
            carry = (
                values * row(a1, level)
                + behind(values) * row(b1, level)
                + (row(d1, level) + row(cl, level, half * ZROWS) * carry)
            )
            field[spot, :] = carry
            return carry

        def down_sweep(i, carry):
            level = CZ - 1 - i
            solved, partial = carry
            spot = pl.ds(pl.multiple_of(base + level * CX, 8), CX)
            solved = field[spot, :] + row(el, level, half * ZROWS) * solved
            partial = solved * row(a2, level) + behind(solved) * row(b2, level) + row(cu, level, half * ZROWS) * partial
            field[spot, :] = partial
            return solved, partial

        def last_sweep(level, carry):
            spot = pl.ds(pl.multiple_of(base + level * CX, 8), CX)
            carry = field[spot, :] + row(eu, level, half * ZROWS) * carry
            field[spot, :] = carry
            eight = carry.reshape(8, 8, HALF)
            here = pl.ds(pl.multiple_of(level * 8, 8), 8)
            part[here, :] = jnp.sum(eight, axis=0)
            partsq[here, :] = jnp.sum(eight * eight, axis=0)
            return carry

        none = jnp.zeros((CX, HALF), jnp.float32)
        lax.fori_loop(0, CZ, up_sweep, none, unroll=UNROLL)
        lax.fori_loop(0, CZ, down_sweep, (none, none), unroll=UNROLL)
        lax.fori_loop(0, CZ, last_sweep, none, unroll=UNROLL)

        def level_sums(ref):
            blocks = []
            for block in range(ZROWS // 8):
                rows = min(8, CZ - 8 * block)
                total = ref[pl.ds(block * 64, rows, stride=8), :]
                for s in range(1, 8):
                    total = total + ref[pl.ds(block * 64 + s, rows, stride=8), :]
                blocks.append(total)
            return jnp.concatenate(blocks, axis=0) * (1.0 / CX)

        mean_after = level_sums(part)
        spread_after = level_sums(partsq) - mean_after * mean_after
        delta[0:CZ, lanes] = mean_after - mean[levels, :]
        delta[L : L + CZ, lanes] = spread_after - spread[levels, :]
        tend = product(delta[:, lanes], weights[...], 0, 0)
        reply[half * N // 2 : (half + 1) * N // 2] = tend.reshape(N // 2, 2, 2 * L)

        targets = [xt * (NZ * NC) + ct for xt in (2 * half, 2 * half + 1) for ct in range(NC)]

        def back(peers, level):
            for plane in peers:
                peer = plane + level * NC
                pltpu.make_async_remote_copy(
                    reply.at[peer], ret.at[me], rep_send, rep_recv, device_id=(peer, strip), device_id_type=MESH
                ).start()

        rings(functools.partial(back, targets))
        for plane in targets:

            @pl.when(plane + z * NC != me)
            def _(plane=plane):
                back([plane], z)

        @pl.when(x // 2 == half)
        def _():
            pltpu.make_async_copy(reply.at[me], ret.at[me], rep_recv).start()

    def store(column, carry):
        spot = lax.rem(column, 8) * 8 + column // 8
        for half in range(2):
            blocks = []
            for block in range(ZROWS // 8):
                rows = min(8, CZ - 8 * block)
                blocks.append(field[pl.ds(half * HROWS + block * 8 * CX + spot, rows, stride=CX), :])
            start = pl.multiple_of(column * SLOTS + half * HALF, HALF)
            out[0, 0, :, pl.ds(start, HALF)] = jnp.concatenate(blocks, axis=0).astype(jnp.bfloat16)
        return carry

    lax.fori_loop(0, CX, store, 0)

    pltpu.make_async_copy(ret, ret, rep_recv).wait()
    both = lax.dot_general(
        picks, split(ret[...].reshape(SLOTS, 2 * L)), (((0,), (0,)), ((), ())), preferred_element_type=jnp.float32
    )
    new[0, :, 0 : 2 * L] = new[0, :, 0 : 2 * L] + (both[:, 0 : 2 * L] + both[:, 2 * L :])
    sent = send.at[pl.ds(0, N - 1)]
    pltpu.make_async_copy(sent, sent, fwd_send).wait()
    pltpu.make_async_copy(sent, sent, rep_send).wait()

def ship(new, out, new_hbm, out_hbm, sems):
    pieces = 8
    width = CX * SLOTS // pieces
    copies = [pltpu.make_async_copy(new, new_hbm, sems.at[pieces])]
    for i in range(pieces):
        lanes = pl.ds(i * width, width)
        copies.append(pltpu.make_async_copy(out.at[0, 0, :, lanes], out_hbm.at[0, 0, :, lanes], sems.at[i]))
    for copy in copies:
        copy.start()
    for copy in copies:
        copy.wait()


def shards(state, owners, orient, crm_state, active_levels, vertical_map, diffusion):
    f32 = jnp.float32
    anywhere = pl.BlockSpec(memory_space=pl.ANY)
    level_rows = pltpu.VMEM((2 * ZROWS, HALF), f32)
    half_rows = pltpu.VMEM((ZROWS, HALF), f32)
    chunks = pltpu.VMEM((N, 2, 2 * L), f32)
    dma = pltpu.SemaphoreType.DMA
    new, out = pl.pallas_call(
        kernel,
        out_shape=(
            pltpu.VMEM(state.shape, f32),
            pltpu.VMEM(crm_state.shape, jnp.bfloat16),
        ),
        in_specs=[anywhere] * 7,
        out_specs=(pl.BlockSpec(memory_space=pltpu.VMEM),) * 2,
        scratch_shapes=[
            pltpu.VMEM((2 * TW + CPD, FL), f32),
            pltpu.VMEM((2, TW, FL), f32),
            pltpu.VMEM((1, CPD), jnp.int32),
            pltpu.VMEM((1, SLOTS), jnp.int32),
            pltpu.VMEM((CZ, L), f32),
            pltpu.SMEM((1, 2), jnp.int32),
            pltpu.SMEM((1, CZ - 1), f32),
            pltpu.VMEM((CZ, CX * SLOTS), jnp.bfloat16),
            pltpu.VMEM((2 * HROWS, HALF), f32),
            *[level_rows] * 6,
            *[half_rows] * 5,
            *[level_rows] * 2,
            pltpu.VMEM((ZROWS * 8, HALF), f32),
            pltpu.VMEM((ZROWS * 8, HALF), f32),
            pltpu.VMEM((CPD, CPD), f32),
            pltpu.VMEM((CPD, SLOTS), f32),
            chunks,
            chunks,
            chunks,
            chunks,
            pltpu.SemaphoreType.REGULAR,
            dma((6,)),
            dma((4,)),
            dma((4,)),
            dma((4,)),
            dma,
            dma((2,)),
            dma,
            dma,
        ],
        compiler_params=pltpu.CompilerParams(collective_id=0, has_side_effects=True, vmem_limit_bytes=56 << 20),
    )(
        state,
        owners.reshape(1, CPD),
        orient.reshape(1, 2),
        crm_state,
        active_levels.reshape(1, SLOTS),
        vertical_map,
        diffusion.reshape(1, CZ - 1),
    )
    return pl.pallas_call(
        ship,
        out_shape=(
            pltpu.HBM(state.shape, f32),
            pltpu.HBM(crm_state.shape, jnp.bfloat16),
        ),
        in_specs=[anywhere] * 2,
        out_specs=(pl.BlockSpec(memory_space=pltpu.HBM),) * 2,
        scratch_shapes=[dma((9,))],
        compiler_params=pltpu.CompilerParams(vmem_limit_bytes=8 << 20),
    )(new, out)


def solution(mesh):
    in_specs = (
        P("edge", "cols", None),
        P("edge", "cols", None),
        P("edge", "cols", None),
        P("edge", "cols", None, None),
        P("edge", "cols", None),
        P(),
        P(),
    )
    out_specs = (P("edge", "cols", None), P("edge", "cols", None, None))
    return jax.shard_map(shards, mesh=mesh, in_specs=in_specs, out_specs=out_specs, check_vma=False)
```
